32 devices in a mesh: node: 8 (over y, x, core), local: 4 (over z).
Axes of the slice: x: 2, y: 2, z: 4, core: 2. Of those that a mesh axis runs over, the one named last changes fastest.
Arguments:
- tokens: bfloat16 [8192, 8192], P(('node', 'local')), may hold values from -6 to 6
- grad_hidden: bfloat16 [8192, 256], P(('node', 'local')), may hold values from -0.0625 to 0.0625
- gate_pre: bfloat16 [8192, 256], P(('node', 'local')), may hold values from -6 to 6
- momentum: float32 [8192, 256], P('local'), may hold values from -6 to 6
Outputs:
- momentum_new: float32 [8192, 256], P('local')
The draws below stay inside these ranges and needn't reach their ends.
All inputs are finite; a program needn't handle non-finite values.
Results may differ from the reference program's by a relative error of at most 0.012.
Values may be sent and summed in bfloat16 or wider, within the bound.
No kernel may reach another device: no remote copies, remote signals or barrier semaphores. Data moves between devices by JAX's collectives and lax.ppermute only.
A program may use at most 64 MiB of HBM per device.

```python
import jax
import jax.numpy as jnp
from jax import lax

D = 8192
COLS = 256
TOK_DEV = 256
TOKENS = 8192
N_NODE = 8
N_LOCAL = 4


def shard_levels(rng, shape, pieces, smallest, largest):
    def one(position, blocks):
        draws = jax.random.uniform(jax.random.fold_in(jax.random.fold_in(rng, 6), position), (blocks,), jnp.float32, smallest / len(pieces), largest / len(pieces))
        return jnp.repeat(jnp.exp(draws), shape[position] // blocks).reshape((-1,) + (1,) * (len(shape) - position - 1))

    factor_of = one(*pieces[0])
    for cut in pieces[1:]:
        factor_of = factor_of * one(*cut)
    return factor_of


def gaussian(rng, extent, spread, bound, cuts=(), dtype=jnp.bfloat16):
    array = spread * jax.random.normal(rng, extent, jnp.float32)
    if cuts:
        array = array * shard_levels(rng, extent, cuts, -0.22, 0.18)
    return jnp.clip(array, -bound, bound).astype(dtype)


def setup_inputs(seed: int = 0) -> dict:
    seeds = jax.random.split(jax.random.key(seed), 5)
    return {
        "tokens": gaussian(seeds[0], (TOKENS, D), 1.0, 6.0, ((0, 32),)),
        "grad_hidden": gaussian(seeds[1], (TOKENS, COLS), TOKENS ** -0.5, 0.0625, ((0, 32),)),
        "gate_pre": gaussian(seeds[2], (TOKENS, COLS), 1.0, 6.0, ((0, 32),)),
        "momentum": gaussian(seeds[3], (D, COLS), 1.0, 6.0, ((0, 4),), jnp.float32),
    }


def reference(tokens, grad_hidden, gate_pre, momentum):
    up_grad = (grad_hidden.astype(jnp.float32) * jax.nn.silu(gate_pre.astype(jnp.float32))).astype(jnp.bfloat16)
    token_groups = tokens.reshape(N_NODE, N_LOCAL, TOK_DEV, D)
    grad_groups = up_grad.reshape(N_NODE, N_LOCAL, TOK_DEV, COLS)

    def local_step(running, pair):
        product = lax.dot_general(pair[0], pair[1], (((0,), (0,)), ((), ())), preferred_element_type=jnp.float32)
        return running + product.astype(jnp.bfloat16).astype(jnp.float32), None

    def node_step(running, pair):
        node_sum, _ = lax.scan(local_step, jnp.zeros((D, COLS), jnp.float32), pair)
        return running + node_sum.astype(jnp.bfloat16).astype(jnp.float32), None

    reduced, _ = lax.scan(node_step, jnp.zeros((D, COLS), jnp.float32), (token_groups, grad_groups))
    return 0.9 * momentum + reduced.astype(jnp.bfloat16).astype(jnp.float32)
```

```python
import functools
import math

import jax
import jax.numpy as jnp
from jax import lax
from jax.experimental import pallas as pl
from jax.experimental.pallas import tpu as pltpu
from jax.sharding import PartitionSpec as P

HBM = pl.BlockSpec(memory_space=pl.ANY)
VMEM = pl.BlockSpec(memory_space=pltpu.VMEM)


def position(side):
    n = lax.axis_index("node")
    core = lax.rem(n, 2)
    chip = lax.div(n, 2)
    return core, lax.rem(chip, side), lax.div(chip, side), lax.axis_index("local")


def place(core, x, y, first, second, side):
    ahead = lax.bitwise_xor(y, jnp.where(core == 0, second, first))
    across = lax.bitwise_xor(x, jnp.where(core == 0, first, second))
    return ahead * side + across


def product_kernel(side, depth, other, up_from_inputs, *refs):
    if up_from_inputs:
        tokens, grad, gate, far, near, up_out, held, done, up_t, in_sems, out_sems = refs
    else:
        tokens, up_in, far, near, held, done, in_sems, out_sems = refs
    core, x, y, z = position(side)
    half = 1 - core if other else core
    block = far.shape[-1]
    chips = side * side
    order = [(f, s, q) for f in range(side - 1, -1, -1) for s in range(side) for q in range(depth)]

    def fetch(i):
        f, s, q = order[i]
        row = (lax.bitwise_xor(z, q) * 2 + half) * chips + place(half, x, y, f, s, side)
        start = pl.multiple_of(row * block, block)
        return pltpu.make_async_copy(tokens.at[:, pl.ds(start, block)], held.at[i], in_sems.at[i])

    def store(i):
        f, s, q = order[i]
        target = near.at[s, q] if f == 0 else far.at[f - 1, s, q]
        return pltpu.make_async_copy(done.at[i], target, out_sems.at[i])

    for i in range(len(order)):
        fetch(i).start()
    if up_from_inputs:
        v = gate[...].astype(jnp.float32)
        up = (grad[...].astype(jnp.float32) * (v * (1.0 / (1.0 + jnp.exp(-v))))).astype(jnp.bfloat16)
        up_t[...] = up.astype(jnp.float32).T.astype(jnp.bfloat16)
        up_out[...] = up_t[...]
        left = up_t
    else:
        left = up_in
    for i in range(len(order)):
        fetch(i).wait()
        done[i] = jnp.dot(left[...], held[i], preferred_element_type=jnp.float32).astype(done.dtype)
        store(i).start()
    for i in range(len(order)):
        store(i).wait()


def products(tokens, ups, other, side, depth, block):
    from_inputs = len(ups) == 2
    token_rows, columns = ups[0].shape if from_inputs else ups[0].shape[::-1]
    count = side * side * depth
    bf16 = jnp.bfloat16
    outs = [
        jax.ShapeDtypeStruct((side - 1, side, depth, columns, block), bf16),
        jax.ShapeDtypeStruct((side, depth, columns, block), bf16),
    ]
    scratch = [pltpu.VMEM((count, token_rows, block), bf16), pltpu.VMEM((count, columns, block), bf16)]
    if from_inputs:
        outs.append(jax.ShapeDtypeStruct((columns, token_rows), bf16))
        scratch.append(pltpu.VMEM((columns, token_rows), bf16))
    return pl.pallas_call(
        functools.partial(product_kernel, side, depth, other, from_inputs),
        out_shape=outs,
        in_specs=[HBM] + [VMEM] * len(ups),
        out_specs=[HBM, HBM] + [VMEM] * from_inputs,
        scratch_shapes=scratch + [pltpu.SemaphoreType.DMA((count,)), pltpu.SemaphoreType.DMA((count,))],
        name="products_other" if other else "products_own",
    )(tokens, *ups)


def turn_kernel(*refs):
    *parts, out = refs
    total = parts[0][...].astype(jnp.float32)
    for part in parts[1:]:
        total += part[...].astype(jnp.float32)
    out[...] = total.T.astype(out.dtype)


def add(a, b):
    return (a.astype(jnp.float32) + b.astype(jnp.float32)).astype(jnp.bfloat16)


def fast(side, depth, tokens, grad_hidden, gate_pre, momentum):
    nodes = 2 * side * side
    block = momentum.shape[0] // nodes

    def chip_pairs(first, second):
        pairs = []
        for n in range(nodes):
            core, x, y = n % 2, n // 2 % side, n // 2 // side
            dx, dy = (first, second) if core == 0 else (second, first)
            pairs.append((n, ((y ^ dy) * side + (x ^ dx)) * 2 + core))
        return pairs

    cores = [(n, n ^ 1) for n in range(nodes)]

    far, near, up_t = products(tokens, (grad_hidden, gate_pre), True, side, depth, block)
    got_far = lax.ppermute(far, "node", cores)
    got_near = lax.ppermute(near, "node", cores)
    own_far, own_near = products(tokens, (up_t,), False, side, depth, block)

    kept = [own_near, got_near]
    for f in range(1, side):
        kept.append(lax.ppermute(add(own_far[f - 1], got_far[f - 1]), "node", chip_pairs(f, 0)))

    def total(arrays, index):
        out = arrays[0][index].astype(jnp.float32)
        for a in arrays[1:]:
            out = out + a[index].astype(jnp.float32)
        return out.astype(jnp.bfloat16)

    kept2 = [a[0] for a in kept]
    for s in range(1, side):
        kept2.append(lax.ppermute(total(kept, s), "node", chip_pairs(0, s)))
    mine = [total(kept2, 0)]
    for q in range(1, depth):
        mine.append(lax.ppermute(total(kept2, q), "local", [(i, i ^ q) for i in range(depth)]))

    columns = grad_hidden.shape[1]
    shard = pl.pallas_call(
        turn_kernel,
        out_shape=jax.ShapeDtypeStruct((block, columns), jnp.bfloat16),
        in_specs=[VMEM] * len(mine),
        out_specs=VMEM,
        name="turn",
    )(*mine)

    core, x, y, _ = position(side)
    out = 0.9 * momentum
    pieces = []
    for f in range(side):
        for s in range(side):
            piece = shard if f == s == 0 else lax.ppermute(shard, "node", chip_pairs(f, s))
            pieces.append((core, f, s, piece))
    for _, f, s, piece in list(pieces):
        pieces.append((1 - core, f, s, lax.ppermute(piece, "node", cores)))
    for c, f, s, piece in pieces:
        start = (c * side * side + place(c, x, y, f, s, side)) * block
        old = lax.dynamic_slice(out, (start, 0), (block, columns))
        out = lax.dynamic_update_slice(out, old + piece.astype(jnp.float32), (start, 0))
    return out


def plain(tokens, grad_hidden, gate_pre, momentum):
    up_grad = (grad_hidden.astype(jnp.float32) * jax.nn.silu(gate_pre.astype(jnp.float32))).astype(
        jnp.bfloat16
    )
    owned_rows = momentum.shape[0]
    columns = up_grad.shape[1]
    node_total = lax.psum_scatter(
        lax.dot_general(
            tokens, up_grad, (((0,), (0,)), ((), ())), preferred_element_type=jnp.float32
        ).astype(jnp.bfloat16),
        "local",
        scatter_dimension=0,
        tiled=True,
    )
    nodes = lax.axis_size("node")
    span = owned_rows // nodes
    reduced = jnp.sum(
        lax.all_to_all(
            node_total.reshape(nodes, span, columns),
            "node",
            split_axis=0,
            concat_axis=0,
            tiled=True,
        ).astype(jnp.float32),
        axis=0,
    )
    shard = reduced.astype(jnp.bfloat16)
    gathered = lax.all_gather(shard, "node", axis=0, tiled=True)
    return 0.9 * momentum + gathered.astype(jnp.float32)


def solution(mesh):
    nodes, depth = mesh.shape["node"], mesh.shape["local"]
    side = math.isqrt(nodes // 2)
    square = nodes == 2 * side * side and side & (side - 1) == 0 and depth & (depth - 1) == 0

    def per_device(tokens, grad_hidden, gate_pre, momentum):
        lanes = 128
        aligned = momentum.shape[0] % (nodes * lanes) == 0 and grad_hidden.shape[1] % lanes == 0
        if square and aligned:
            return fast(side, depth, tokens, grad_hidden, gate_pre, momentum)
        return plain(tokens, grad_hidden, gate_pre, momentum)

    in_specs = (
        P(("node", "local"), None),
        P(("node", "local"), None),
        P(("node", "local"), None),
        P("local", None),
    )
    return jax.shard_map(
        per_device, mesh=mesh, in_specs=in_specs, out_specs=P("local", None), check_vma=False
    )
```

```python
import functools
import math

import jax
import jax.numpy as jnp
from jax import lax
from jax.experimental import pallas as pl
from jax.experimental.pallas import tpu as pltpu
from jax.sharding import PartitionSpec as P

HBM = pl.BlockSpec(memory_space=pl.ANY)
VMEM = pl.BlockSpec(memory_space=pltpu.VMEM)
PARAMS = pltpu.CompilerParams(vmem_limit_bytes=12 << 20)


def near(x):
    return pltpu.with_memory_space_constraint(x, pltpu.VMEM)


def position(side):
    n = lax.axis_index("node")
    chip = lax.div(n, 2)
    return lax.rem(n, 2), lax.rem(chip, side), lax.div(chip, side), lax.axis_index("local")


def place(core, x, y, first, second, side):
    ahead = lax.bitwise_xor(y, jnp.where(core == 0, second, first))
    across = lax.bitwise_xor(x, jnp.where(core == 0, first, second))
    return ahead * side + across


def product_kernel(side, depth, other, firsts, streams, width, from_inputs, added, *refs):
    refs = list(refs)
    tokens = refs.pop(0)
    if from_inputs:
        grad, gate = refs.pop(0), refs.pop(0)
    else:
        left_ref = refs.pop(0)
    addends = [refs.pop(0) for _ in streams] if added else []
    outs = [refs.pop(0) for _ in streams]
    if from_inputs:
        left_ref = refs.pop(0)
    held, sems = refs
    core, x, y, z = position(side)
    half = 1 - core if other else core
    chips = side * side
    span = width * len(streams)
    block = tokens.shape[1] // (2 * chips * depth)
    order = [(f, s, q) for f in firsts for s in range(side) for q in range(depth)]

    copies = []
    for i, (f, s, q) in enumerate(order):
        row = (lax.bitwise_xor(z, q) * 2 + half) * chips + place(half, x, y, f, s, side)
        start = pl.multiple_of(row * block + streams[0] * width, width)
        copies.append(
            pltpu.make_async_copy(tokens.at[:, pl.ds(start, span)], held.at[:, pl.ds(i * span, span)], sems.at[i])
        )
    for copy in copies:
        copy.start()
    if from_inputs:
        v = gate[...].astype(jnp.float32)
        up = grad[...].astype(jnp.float32) * (v / (1.0 + jnp.exp(-v)))
        left_ref[...] = up.astype(jnp.bfloat16).T
    left = left_ref[...]
    for copy in copies:
        copy.wait()
    together = max(1, 256 // span)
    for base in range(0, len(order), together):
        group = order[base : base + together]
        columns = pl.ds(base * span, span * len(group))
        result = jnp.dot(left, held[:, columns], preferred_element_type=jnp.float32)
        for j, (f, s, q) in enumerate(group):
            for u in range(len(streams)):
                at = (f - firsts[0], s, q)
                lane = (j * len(streams) + u) * width
                value = result[:, lane : lane + width]
                if added:
                    value = value + addends[u][at].astype(jnp.float32)
                outs[u][at] = value.astype(jnp.bfloat16)


def products(tokens, ups, addends, other, firsts, streams, side, depth, width):
    from_inputs = len(ups) == 2
    token_rows, columns = ups[0].shape if from_inputs else ups[0].shape[::-1]
    count = len(firsts) * side * depth
    outs = [pltpu.VMEM((len(firsts), side, depth, columns, width), jnp.bfloat16) for _ in streams]
    if from_inputs:
        outs.append(pltpu.VMEM((columns, token_rows), jnp.bfloat16))
    else:
        ups = [near(u) for u in ups]
    addends = [near(a) for a in addends]
    return pl.pallas_call(
        functools.partial(
            product_kernel, side, depth, other, firsts, streams, width, from_inputs, bool(addends)
        ),
        out_shape=outs,
        in_specs=[HBM] + [VMEM] * (len(ups) + len(addends)),
        out_specs=[VMEM] * len(outs),
        scratch_shapes=[
            pltpu.VMEM((token_rows, count * width * len(streams)), jnp.bfloat16),
            pltpu.SemaphoreType.DMA((count,)),
        ],
        compiler_params=PARAMS,
        name="products",
    )(tokens, *ups, *addends)


def turn_kernel(*refs):
    *parts, out = refs
    total = parts[0][...].astype(jnp.float32)
    for part in parts[1:]:
        total += part[...].astype(jnp.float32)
    out[...] = total.T.astype(out.dtype)


def update_kernel(side, places, stream, width, *refs):
    momentum, *pieces = refs[: 1 + len(places)]
    out, held, sems = refs[-3:]
    core, x, y, _ = position(side)
    block = momentum.shape[0] // (2 * side * side)
    copies = []
    for i, (swapped, f, s) in enumerate(places):
        c = 1 - core if swapped else core
        start = (c * side * side + place(c, x, y, f, s, side)) * block + stream * width
        rows = pl.ds(pl.multiple_of(start, width), width)
        held[i] = 0.9 * momentum[rows, :] + pieces[i][...].astype(jnp.float32)
        copies.append(pltpu.make_async_copy(held.at[i], out.at[rows, :], sems.at[i]))
        copies[-1].start()
    for copy in copies:
        copy.wait()


def update(out, momentum, pieces, places, stream, side, width):
    again = [] if out is None else [out]
    columns = momentum.shape[1]
    return pl.pallas_call(
        functools.partial(update_kernel, side, places, stream, width),
        out_shape=jax.ShapeDtypeStruct(momentum.shape, momentum.dtype),
        in_specs=[VMEM] * (1 + len(pieces)) + [HBM] * len(again),
        out_specs=HBM,
        input_output_aliases={1 + len(pieces): 0} if again else {},
        scratch_shapes=[
            pltpu.VMEM((len(pieces), width, columns), jnp.float32),
            pltpu.SemaphoreType.DMA((len(pieces),)),
        ],
        compiler_params=PARAMS,
        name="update",
    )(near(momentum), *[near(p) for p in pieces], *again)


def fast(side, depth, parts, tokens, grad_hidden, gate_pre, momentum):
    nodes = 2 * side * side
    width = momentum.shape[0] // nodes // parts
    columns = grad_hidden.shape[1]
    streams = list(range(parts))
    far_firsts, near_firsts = list(range(1, side)), [0]

    def chip_pairs(first, second):
        pairs = []
        for n in range(nodes):
            core, x, y = n % 2, n // 2 % side, n // 2 // side
            dx, dy = (first, second) if core == 0 else (second, first)
            pairs.append((n, ((y ^ dy) * side + (x ^ dx)) * 2 + core))
        return pairs

    cores = [(n, n ^ 1) for n in range(nodes)]

    def total(arrays, index):
        out = arrays[0][index].astype(jnp.float32)
        for a in arrays[1:]:
            out = out + a[index].astype(jnp.float32)
        return out.astype(jnp.bfloat16)

    def multiply(tokens, ups, addends, other, firsts, of):
        return products(tokens, ups, addends, other, firsts, of, side, depth, width)

    first_far, up_t = multiply(tokens, (grad_hidden, gate_pre), [], True, far_firsts, [0])
    far = [first_far] + [multiply(tokens, (up_t,), [], True, far_firsts, [u])[0] for u in streams[1:]]
    far = [lax.ppermute(a, "node", cores) for a in far]
    held = []
    for u in streams:
        summed = multiply(tokens, (up_t,), [far[u]], False, far_firsts, [u])[0]
        held.append([lax.ppermute(summed[f - 1], "node", chip_pairs(f, 0)) for f in range(1, side)])
    close = multiply(tokens, (up_t,), [], True, near_firsts, streams)
    close = [lax.ppermute(a, "node", cores) for a in close]
    kept = multiply(tokens, (up_t,), close, False, near_firsts, streams)

    held = [[kept[u][0]] + held[u] for u in streams]
    for u in streams:
        sent = [lax.ppermute(total(held[u], s), "node", chip_pairs(0, s)) for s in range(1, side)]
        held[u] = [a[0] for a in held[u]] + sent
    for u in streams:
        held[u] = [total(held[u], 0)] + [
            lax.ppermute(total(held[u], q), "local", [(i, i ^ q) for i in range(depth)])
            for q in range(1, depth)
        ]
    out = None
    for u in streams:
        shard = pl.pallas_call(
            turn_kernel,
            out_shape=pltpu.VMEM((width, columns), jnp.bfloat16),
            in_specs=[VMEM] * depth,
            out_specs=VMEM,
            compiler_params=PARAMS,
            name="turn",
        )(*[near(a) for a in held[u]])
        places = [(f, s) for f in range(side) for s in range(side)]
        pieces = [shard if f == s == 0 else lax.ppermute(shard, "node", chip_pairs(f, s)) for f, s in places]
        pieces += [lax.ppermute(a, "node", cores) for a in pieces]
        places = [(False, f, s) for f, s in places] + [(True, f, s) for f, s in places]
        out = update(out, momentum, pieces, places, u, side, width)
    return out


def plain(tokens, grad_hidden, gate_pre, momentum):
    up_grad = (grad_hidden.astype(jnp.float32) * jax.nn.silu(gate_pre.astype(jnp.float32))).astype(
        jnp.bfloat16
    )
    owned_rows = momentum.shape[0]
    columns = up_grad.shape[1]
    node_total = lax.psum_scatter(
        lax.dot_general(
            tokens, up_grad, (((0,), (0,)), ((), ())), preferred_element_type=jnp.float32
        ).astype(jnp.bfloat16),
        "local",
        scatter_dimension=0,
        tiled=True,
    )
    nodes = lax.axis_size("node")
    span = owned_rows // nodes
    reduced = jnp.sum(
        lax.all_to_all(
            node_total.reshape(nodes, span, columns),
            "node",
            split_axis=0,
            concat_axis=0,
            tiled=True,
        ).astype(jnp.float32),
        axis=0,
    )
    shard = reduced.astype(jnp.bfloat16)
    gathered = lax.all_gather(shard, "node", axis=0, tiled=True)
    return 0.9 * momentum + gathered.astype(jnp.float32)


def solution(mesh):
    nodes, depth = mesh.shape["node"], mesh.shape["local"]
    side = math.isqrt(nodes // 2)
    square = nodes == 2 * side * side and side & (side - 1) == 0 and depth & (depth - 1) == 0

    def per_device(tokens, grad_hidden, gate_pre, momentum):
        lanes = 128
        aligned = momentum.shape[0] % (nodes * lanes) == 0 and grad_hidden.shape[1] % lanes == 0
        if square and aligned:
            parts = 2 if momentum.shape[0] % (2 * nodes * lanes) == 0 else 1
            return fast(side, depth, parts, tokens, grad_hidden, gate_pre, momentum)
        return plain(tokens, grad_hidden, gate_pre, momentum)

    in_specs = (
        P(("node", "local"), None),
        P(("node", "local"), None),
        P(("node", "local"), None),
        P("local", None),
    )
    return jax.shard_map(
        per_device, mesh=mesh, in_specs=in_specs, out_specs=P("local", None), check_vma=False
    )
```

```python
import functools
import math

import jax
import jax.numpy as jnp
from jax import lax
from jax.experimental import pallas as pl
from jax.experimental.pallas import tpu as pltpu
from jax.sharding import PartitionSpec as P


ANY = pl.BlockSpec(memory_space=pl.ANY)
HBM = pl.BlockSpec(memory_space=pltpu.HBM)
VMEM = pl.BlockSpec(memory_space=pltpu.VMEM)
PARAMS = pltpu.CompilerParams(vmem_limit_bytes=12 << 20)


def near(x):
    return pltpu.with_memory_space_constraint(x, pltpu.VMEM)


def far_off(x):
    return pltpu.with_memory_space_constraint(x, pltpu.HBM)


def after(values, *others):
    return lax.optimization_barrier((values, others))[0]


def position(side):
    n = lax.axis_index("node")
    chip = lax.div(n, 2)
    return lax.rem(n, 2), lax.rem(chip, side), lax.div(chip, side), lax.axis_index("local")


def place(core, x, y, first, second, side):
    ahead = lax.bitwise_xor(y, jnp.where(core == 0, second, first))
    across = lax.bitwise_xor(x, jnp.where(core == 0, first, second))
    return ahead * side + across


def product_kernel(side, depth, other, groups, part, from_inputs, added, *refs):
    refs = list(refs)
    tokens = refs.pop(0)
    if from_inputs:
        grad, gate = refs.pop(0), refs.pop(0)
    else:
        left_ref = refs.pop(0)
    addend = refs.pop(0) if added else None
    outs = [refs.pop(0) for _ in groups]
    if from_inputs:
        left_ref = refs.pop(0)
    held, sems = refs[:2]
    core, x, y, z = position(side)
    half = 1 - core if other else core
    chips = side * side
    block = tokens.shape[1] // (2 * chips * depth)
    order = [(g, j, at) for g, group in enumerate(groups) for j, at in enumerate(group)]

    copies = []
    for i, (_, _, (f, s, q)) in enumerate(order):
        row = (lax.bitwise_xor(z, q) * 2 + half) * chips + place(half, x, y, f, s, side)
        start = pl.multiple_of(row * block, block)
        copies.append(
            pltpu.make_async_copy(tokens.at[:, pl.ds(start, block)], held.at[:, pl.ds(i * block, block)], sems.at[i])
        )
    if from_inputs:
        small = [pltpu.make_async_copy(a, refs[2].at[i], refs[3].at[i]) for i, a in enumerate((grad, gate))]
        for copy in small:
            copy.start()
    for copy in copies:
        copy.start()
    if from_inputs:
        for copy in small:
            copy.wait()
        v = refs[2][1].astype(jnp.float32)
        up = refs[2][0].astype(jnp.float32) * (v / (1.0 + jnp.exp(-v)))
        left_ref[...] = up.astype(jnp.bfloat16).T
    left = left_ref[part[0] : part[1], :]
    for copy in copies:
        copy.wait()
    for i, (g, j, _) in enumerate(order):
        value = jnp.dot(left, held[:, pl.ds(i * block, block)], preferred_element_type=jnp.float32)
        if added:
            value = value + addend[i].astype(jnp.float32)
        outs[g][j] = value.astype(jnp.bfloat16)


def products(tokens, ups, addend, other, groups, part, side, depth, block):
    from_inputs = len(ups) == 2
    token_rows, columns = ups[0].shape if from_inputs else ups[0].shape[::-1]
    count = sum(len(group) for group in groups)
    outs = [pltpu.VMEM((len(group), part[1] - part[0], block), jnp.bfloat16) for group in groups]
    if from_inputs:
        outs.append(pltpu.VMEM((columns, token_rows), jnp.bfloat16))
        tokens, ups = far_off(tokens), [far_off(u) for u in ups]
        extra = [pltpu.VMEM((2, *ups[0].shape), ups[0].dtype), pltpu.SemaphoreType.DMA((2,))]
    else:
        tokens, ups = near(tokens), [near(u) for u in ups]
        extra = []
    addends = [] if addend is None else [near(addend)]
    return pl.pallas_call(
        functools.partial(product_kernel, side, depth, other, groups, part, from_inputs, bool(addends)),
        out_shape=outs,
        in_specs=[HBM if from_inputs else VMEM] * (1 + len(ups)) + [VMEM] * len(addends),
        out_specs=[VMEM] * len(outs),
        scratch_shapes=[
            pltpu.VMEM((token_rows, count * block), jnp.bfloat16),
            pltpu.SemaphoreType.DMA((count,)),
            *extra,
        ],
        compiler_params=PARAMS,
        name="products",
    )(tokens, *ups, *addends)


def update_kernel(side, swapped, *refs):
    chips = side * side
    momentum, wide, *pieces = refs[: 2 + chips]
    out, held, sems = refs[-3:]
    core, x, y, _ = position(side)
    block = momentum.shape[0] // (2 * chips)
    c = 1 - core if swapped else core
    copies = []
    for i in range(chips):
        start = (c * chips + place(c, x, y, i // side, i % side, side)) * block
        rows = pl.ds(pl.multiple_of(start, block), block)
        reduced = jnp.concatenate([wide[i], pieces[i][...]], axis=0)
        held[i] = momentum[rows, :] + reduced.T.astype(jnp.float32)
        copies.append(pltpu.make_async_copy(held.at[i], out.at[rows, :], sems.at[i]))
        copies[-1].start()
    for copy in copies:
        copy.wait()


def update(out, momentum, wide, pieces, swapped, side):
    again = [] if out is None else [out]
    rows, columns = momentum.shape
    chips = len(pieces)
    return pl.pallas_call(
        functools.partial(update_kernel, side, swapped),
        out_shape=jax.ShapeDtypeStruct(momentum.shape, momentum.dtype),
        in_specs=[VMEM] * (2 + chips) + [HBM] * len(again),
        out_specs=HBM,
        input_output_aliases={2 + chips: 0} if again else {},
        scratch_shapes=[
            pltpu.VMEM((chips, rows // (2 * chips), columns), jnp.float32),
            pltpu.SemaphoreType.DMA((chips,)),
        ],
        compiler_params=PARAMS,
        name="update",
    )(near(momentum), near(wide), *[near(p) for p in pieces], *again)


def gathered_kernel(side, *refs):
    *parts, out = refs
    for i in range(len(parts)):
        value = None
        for k, part in enumerate(parts):
            f, s = i // side ^ k // side, i % side ^ k % side
            addend = part[f * side + s].astype(jnp.float32)
            value = addend if value is None else value + addend
        out[i] = value.astype(out.dtype)


def gathered(parts, side):
    return pl.pallas_call(
        functools.partial(gathered_kernel, side),
        out_shape=pltpu.VMEM(parts[0].shape, parts[0].dtype),
        in_specs=[VMEM] * len(parts),
        out_specs=VMEM,
        compiler_params=PARAMS,
        name="gathered",
    )(*[near(p) for p in parts])


def total(parts):
    out = parts[0].astype(jnp.float32)
    for part in parts[1:]:
        out = out + part.astype(jnp.float32)
    return out.astype(jnp.bfloat16)


def fast(side, depth, wide_columns, tokens, grad_hidden, gate_pre, momentum):
    nodes = 2 * side * side
    block = momentum.shape[0] // nodes
    columns = grad_hidden.shape[1]
    sides, depths = range(side), range(depth)
    wide_part, part = (0, wide_columns), (wide_columns, columns)

    def chip_pairs(first, second):
        pairs = []
        for n in range(nodes):
            core, x, y = n % 2, n // 2 % side, n // 2 // side
            dx, dy = (first, second) if core == 0 else (second, first)
            pairs.append((n, ((y ^ dy) * side + (x ^ dx)) * 2 + core))
        return pairs

    def swap(a):
        return lax.ppermute(a, "node", [(n, n ^ 1) for n in range(nodes)])

    def plane(a, first, second):
        return lax.ppermute(a, "node", chip_pairs(first, second))

    def along(a, q):
        return lax.ppermute(a, "local", [(i, i ^ q) for i in depths])

    def flat(groups):
        return [[at for group in groups for at in group]]

    def multiply(tokens, ups, addend, other, groups, of):
        return products(tokens, ups, addend, other, groups, of, side, depth, block)

    far = [[(f, s, q) for s in sides for q in depths] for f in range(1, side)]
    close = [[(0, s, q) for s in sides for q in depths]]
    wide = [[(f, s, q) for f in sides for s in sides] for q in depths]

    far_other, up_t = multiply(tokens, (grad_hidden, gate_pre), None, True, flat(far), part)
    far_got = swap(far_other)
    wide_other = multiply(tokens, (up_t,), None, True, flat(wide), wide_part)[0]
    wide_got = swap(wide_other)
    far_sum = multiply(tokens, (up_t,), far_got, False, far, part)
    held = [plane(a, f, 0) for f, a in enumerate(far_sum, 1)]
    wide_sum = multiply(tokens, (up_t,), wide_got, False, wide, wide_part)
    wide_held = [wide_sum[0]] + [along(wide_sum[q], q) for q in range(1, depth)]
    close_up = after(up_t, wide_other, *far_sum)
    close_other = multiply(tokens, (close_up,), None, True, close, part)[0]
    close_got = swap(close_other)
    held = [*multiply(tokens, (close_up,), close_got, False, close, part), *held]

    sent = [plane(total([a[s * depth : (s + 1) * depth] for a in held]), 0, s) for s in range(1, side)]
    held = [a[:depth] for a in held] + sent
    pieces = [total([a[q] for a in held]) for q in depths]
    wide_held = after(wide_held, *pieces[1:])
    shard = total([pieces[0]] + [along(pieces[q], q) for q in range(1, depth)])

    places = [(f, s) for f in sides for s in sides]
    wide_shard = total(wide_held)
    wide_all = [wide_shard if at == (0, 0) else plane(wide_shard, *at) for at in places]
    own = [shard if at == (0, 0) else plane(shard, *at) for at in places]
    decayed = 0.9 * momentum
    wide_own = gathered(wide_all, side)
    out = update(None, decayed, wide_own, own, False, side)
    return update(out, decayed, swap(wide_own), [swap(a) for a in own], True, side)


def plain(tokens, grad_hidden, gate_pre, momentum):
    up_grad = (grad_hidden.astype(jnp.float32) * jax.nn.silu(gate_pre.astype(jnp.float32))).astype(
        jnp.bfloat16
    )
    owned_rows = momentum.shape[0]
    columns = up_grad.shape[1]
    node_total = lax.psum_scatter(
        lax.dot_general(
            tokens, up_grad, (((0,), (0,)), ((), ())), preferred_element_type=jnp.float32
        ).astype(jnp.bfloat16),
        "local",
        scatter_dimension=0,
        tiled=True,
    )
    nodes = lax.axis_size("node")
    span = owned_rows // nodes
    reduced = jnp.sum(
        lax.all_to_all(
            node_total.reshape(nodes, span, columns),
            "node",
            split_axis=0,
            concat_axis=0,
            tiled=True,
        ).astype(jnp.float32),
        axis=0,
    )
    shard = reduced.astype(jnp.bfloat16)
    gathered = lax.all_gather(shard, "node", axis=0, tiled=True)
    return 0.9 * momentum + gathered.astype(jnp.float32)


def solution(mesh):
    nodes, depth = mesh.shape["node"], mesh.shape["local"]
    side = math.isqrt(nodes // 2)
    square = nodes == 2 * side * side and side & (side - 1) == 0 and depth & (depth - 1) == 0

    def per_device(tokens, grad_hidden, gate_pre, momentum):
        lanes = 128
        aligned = momentum.shape[0] % (nodes * lanes) == 0 and grad_hidden.shape[1] % lanes == 0
        if square and aligned:
            wide = grad_hidden.shape[1] * 3 // 8 // 16 * 16
            return fast(side, depth, wide, tokens, grad_hidden, gate_pre, momentum)
        return plain(tokens, grad_hidden, gate_pre, momentum)

    in_specs = (
        P(("node", "local"), None),
        P(("node", "local"), None),
        P(("node", "local"), None),
        P("local", None),
    )
    return jax.shard_map(
        per_device, mesh=mesh, in_specs=in_specs, out_specs=P("local", None), check_vma=False
    )
```

```python
import functools
import math

import jax
import jax.numpy as jnp
from jax import lax
from jax.experimental import pallas as pl
from jax.experimental.pallas import tpu as pltpu
from jax.sharding import PartitionSpec as P


ANY = pl.BlockSpec(memory_space=pl.ANY)
HBM = pl.BlockSpec(memory_space=pltpu.HBM)
VMEM = pl.BlockSpec(memory_space=pltpu.VMEM)
PARAMS = pltpu.CompilerParams(vmem_limit_bytes=12 << 20)


def near(x):
    return pltpu.with_memory_space_constraint(x, pltpu.VMEM)


def far_off(x):
    return pltpu.with_memory_space_constraint(x, pltpu.HBM)


def after(values, *others):
    return lax.optimization_barrier((values, others))[0]


def position(side):
    n = lax.axis_index("node")
    chip = lax.div(n, 2)
    return lax.rem(n, 2), lax.rem(chip, side), lax.div(chip, side), lax.axis_index("local")


def place(core, x, y, first, second, side):
    ahead = lax.bitwise_xor(y, jnp.where(core == 0, second, first))
    across = lax.bitwise_xor(x, jnp.where(core == 0, first, second))
    return ahead * side + across


def product_kernel(side, depth, other, groups, part, from_inputs, added, *refs):
    refs = list(refs)
    tokens = refs.pop(0)
    if from_inputs:
        grad, gate = refs.pop(0), refs.pop(0)
    else:
        left_ref = refs.pop(0)
    addend = refs.pop(0) if added else None
    outs = [refs.pop(0) for _ in groups]
    if from_inputs:
        left_ref = refs.pop(0)
    held, sems = refs[:2]
    core, x, y, z = position(side)
    half = 1 - core if other else core
    chips = side * side
    block = tokens.shape[1] // (2 * chips * depth)
    order = [(g, j, at) for g, group in enumerate(groups) for j, at in enumerate(group)]

    copies = []
    for i, (_, _, (f, s, q)) in enumerate(order):
        row = (lax.bitwise_xor(z, q) * 2 + half) * chips + place(half, x, y, f, s, side)
        start = pl.multiple_of(row * block, block)
        copies.append(
            pltpu.make_async_copy(tokens.at[:, pl.ds(start, block)], held.at[:, pl.ds(i * block, block)], sems.at[i])
        )
    if from_inputs:
        small = [pltpu.make_async_copy(a, refs[2].at[i], refs[3].at[i]) for i, a in enumerate((grad, gate))]
        for copy in small:
            copy.start()
    for copy in copies:
        copy.start()
    if from_inputs:
        for copy in small:
            copy.wait()
        v = refs[2][1].astype(jnp.float32)
        up = refs[2][0].astype(jnp.float32) * (v / (1.0 + jnp.exp(-v)))
        left_ref[...] = up.astype(jnp.bfloat16).T
    left = left_ref[part[0] : part[1], :]
    for copy in copies:
        copy.wait()
    for i, (g, j, _) in enumerate(order):
        value = jnp.dot(left, held[:, pl.ds(i * block, block)], preferred_element_type=jnp.float32)
        if added:
            value = value + addend[i].astype(jnp.float32)
        outs[g][j] = value.astype(jnp.bfloat16)


def products(tokens, ups, addend, other, groups, part, side, depth, block):
    from_inputs = len(ups) == 2
    token_rows, columns = ups[0].shape if from_inputs else ups[0].shape[::-1]
    count = sum(len(group) for group in groups)
    outs = [pltpu.VMEM((len(group), part[1] - part[0], block), jnp.bfloat16) for group in groups]
    if from_inputs:
        outs.append(pltpu.VMEM((columns, token_rows), jnp.bfloat16))
        tokens, ups = far_off(tokens), [far_off(u) for u in ups]
        extra = [pltpu.VMEM((2, *ups[0].shape), ups[0].dtype), pltpu.SemaphoreType.DMA((2,))]
    else:
        tokens, ups = near(tokens), [near(u) for u in ups]
        extra = []
    addends = [] if addend is None else [near(addend)]
    return pl.pallas_call(
        functools.partial(product_kernel, side, depth, other, groups, part, from_inputs, bool(addends)),
        out_shape=outs,
        in_specs=[HBM if from_inputs else VMEM] * (1 + len(ups)) + [VMEM] * len(addends),
        out_specs=[VMEM] * len(outs),
        scratch_shapes=[
            pltpu.VMEM((token_rows, count * block), jnp.bfloat16),
            pltpu.SemaphoreType.DMA((count,)),
            *extra,
        ],
        compiler_params=PARAMS,
        name="products",
    )(tokens, *ups, *addends)


def update_kernel(side, swapped, *refs):
    chips = side * side
    momentum, *pieces = refs[: 1 + chips]
    out, held, sems = refs[-3:]
    core, x, y, _ = position(side)
    block = momentum.shape[0] // (2 * chips)
    c = 1 - core if swapped else core
    copies = []
    for i in range(chips):
        start = (c * chips + place(c, x, y, i // side, i % side, side)) * block
        rows = pl.ds(pl.multiple_of(start, block), block)
        held[i] = 0.9 * momentum[rows, :] + pieces[i][...].astype(jnp.float32)
        copies.append(pltpu.make_async_copy(held.at[i], out.at[rows, :], sems.at[i]))
        copies[-1].start()
    for copy in copies:
        copy.wait()


def update(out, momentum, pieces, swapped, side):
    again = [] if out is None else [out]
    rows, columns = momentum.shape
    chips = len(pieces)
    return pl.pallas_call(
        functools.partial(update_kernel, side, swapped),
        out_shape=jax.ShapeDtypeStruct(momentum.shape, momentum.dtype),
        in_specs=[VMEM] * (1 + chips) + [HBM] * len(again),
        out_specs=HBM,
        input_output_aliases={1 + chips: 0} if again else {},
        scratch_shapes=[
            pltpu.VMEM((chips, rows // (2 * chips), columns), jnp.float32),
            pltpu.SemaphoreType.DMA((chips,)),
        ],
        compiler_params=PARAMS,
        name="update",
    )(near(momentum), *[near(p) for p in pieces], *again)


def turned_kernel(wide_parts, *refs):
    *parts, out = refs
    sums = []
    for group in (parts[:wide_parts], parts[wide_parts:]):
        value = group[0][...].astype(jnp.float32)
        for part in group[1:]:
            value += part[...].astype(jnp.float32)
        sums.append(value.astype(out.dtype))
    out[...] = jnp.concatenate(sums, axis=0).T


def turned(wide_parts, parts):
    columns = wide_parts[0].shape[0] + parts[0].shape[0]
    return pl.pallas_call(
        functools.partial(turned_kernel, len(wide_parts)),
        out_shape=pltpu.VMEM((parts[0].shape[1], columns), parts[0].dtype),
        in_specs=[VMEM] * (len(wide_parts) + len(parts)),
        out_specs=VMEM,
        compiler_params=PARAMS,
        name="turned",
    )(*[near(p) for p in (*wide_parts, *parts)])


def total(parts):
    out = parts[0].astype(jnp.float32)
    for part in parts[1:]:
        out = out + part.astype(jnp.float32)
    return out.astype(jnp.bfloat16)


def fast(side, depth, wide_columns, tokens, grad_hidden, gate_pre, momentum):
    nodes = 2 * side * side
    block = momentum.shape[0] // nodes
    columns = grad_hidden.shape[1]
    sides, depths = range(side), range(depth)
    wide_part, part = (0, wide_columns), (wide_columns, columns)

    def chip_pairs(first, second):
        pairs = []
        for n in range(nodes):
            core, x, y = n % 2, n // 2 % side, n // 2 // side
            dx, dy = (first, second) if core == 0 else (second, first)
            pairs.append((n, ((y ^ dy) * side + (x ^ dx)) * 2 + core))
        return pairs

    def swap(a):
        return lax.ppermute(a, "node", [(n, n ^ 1) for n in range(nodes)])

    def plane(a, first, second):
        return lax.ppermute(a, "node", chip_pairs(first, second))

    def along(a, q):
        return lax.ppermute(a, "local", [(i, i ^ q) for i in depths])

    def flat(groups):
        return [[at for group in groups for at in group]]

    def multiply(tokens, ups, addend, other, groups, of):
        return products(tokens, ups, addend, other, groups, of, side, depth, block)

    far = [[(f, s, q) for s in sides for q in depths] for f in range(1, side)]
    close = [[(0, s, q) for s in sides for q in depths]]
    wide = [[(f, s, q) for f in sides for s in sides] for q in depths]

    far_other, up_t = multiply(tokens, (grad_hidden, gate_pre), None, True, flat(far), part)
    far_got = swap(far_other)
    wide_other = multiply(tokens, (up_t,), None, True, flat(wide), wide_part)[0]
    wide_got = swap(wide_other)
    far_sum = multiply(tokens, (up_t,), far_got, False, far, part)
    held = [plane(a, f, 0) for f, a in enumerate(far_sum, 1)]
    wide_sum = multiply(tokens, (up_t,), wide_got, False, wide, wide_part)
    wide_held = [wide_sum[0]] + [along(wide_sum[q], q) for q in range(1, depth)]
    close_up = after(up_t, wide_other, *far_sum)
    close_other = multiply(tokens, (close_up,), None, True, close, part)[0]
    close_got = swap(close_other)
    held = [*multiply(tokens, (close_up,), close_got, False, close, part), *held]

    sent = [plane(total([a[s * depth : (s + 1) * depth] for a in held]), 0, s) for s in range(1, side)]
    held = [a[:depth] for a in held] + sent
    pieces = [total([a[q] for a in held]) for q in depths]
    wide_held = after(wide_held, *pieces[1:])
    pieces = pieces[:1] + [along(pieces[q], q) for q in range(1, depth)]

    places = [(f, s) for f in sides for s in sides]
    blocks = [total([a[i] for a in wide_held]) for i in range(len(places))]
    blocks = blocks[:1] + [plane(a, *at) for a, at in zip(blocks[1:], places[1:])]
    shard = turned(blocks, pieces)
    own = [shard if at == (0, 0) else plane(shard, *at) for at in places]
    out = update(None, momentum, own, False, side)
    return update(out, momentum, [swap(a) for a in own], True, side)


def plain(tokens, grad_hidden, gate_pre, momentum):
    up_grad = (grad_hidden.astype(jnp.float32) * jax.nn.silu(gate_pre.astype(jnp.float32))).astype(
        jnp.bfloat16
    )
    owned_rows = momentum.shape[0]
    columns = up_grad.shape[1]
    node_total = lax.psum_scatter(
        lax.dot_general(
            tokens, up_grad, (((0,), (0,)), ((), ())), preferred_element_type=jnp.float32
        ).astype(jnp.bfloat16),
        "local",
        scatter_dimension=0,
        tiled=True,
    )
    nodes = lax.axis_size("node")
    span = owned_rows // nodes
    reduced = jnp.sum(
        lax.all_to_all(
            node_total.reshape(nodes, span, columns),
            "node",
            split_axis=0,
            concat_axis=0,
            tiled=True,
        ).astype(jnp.float32),
        axis=0,
    )
    shard = reduced.astype(jnp.bfloat16)
    gathered = lax.all_gather(shard, "node", axis=0, tiled=True)
    return 0.9 * momentum + gathered.astype(jnp.float32)


def solution(mesh):
    nodes, depth = mesh.shape["node"], mesh.shape["local"]
    side = math.isqrt(nodes // 2)
    square = nodes == 2 * side * side and side & (side - 1) == 0 and depth & (depth - 1) == 0

    def per_device(tokens, grad_hidden, gate_pre, momentum):
        lanes = 128
        aligned = momentum.shape[0] % (nodes * lanes) == 0 and grad_hidden.shape[1] % lanes == 0
        if square and aligned:
            wide = grad_hidden.shape[1] * 5 // 16 // 16 * 16
            return fast(side, depth, wide, tokens, grad_hidden, gate_pre, momentum)
        return plain(tokens, grad_hidden, gate_pre, momentum)

    in_specs = (
        P(("node", "local"), None),
        P(("node", "local"), None),
        P(("node", "local"), None),
        P("local", None),
    )
    return jax.shard_map(
        per_device, mesh=mesh, in_specs=in_specs, out_specs=P("local", None), check_vma=False
    )
```

```python
import functools
import math

import jax
import jax.numpy as jnp
from jax import lax
from jax.experimental import pallas as pl
from jax.experimental.pallas import tpu as pltpu
from jax.sharding import PartitionSpec as P


ANY = pl.BlockSpec(memory_space=pl.ANY)
HBM = pl.BlockSpec(memory_space=pltpu.HBM)
VMEM = pl.BlockSpec(memory_space=pltpu.VMEM)
PARAMS = pltpu.CompilerParams(vmem_limit_bytes=12 << 20)


def near(x):
    return pltpu.with_memory_space_constraint(x, pltpu.VMEM)


def far_off(x):
    return pltpu.with_memory_space_constraint(x, pltpu.HBM)


def after(values, *others):
    return lax.optimization_barrier((values, others))[0]


def position(side):
    n = lax.axis_index("node")
    chip = lax.div(n, 2)
    return lax.rem(n, 2), lax.rem(chip, side), lax.div(chip, side), lax.axis_index("local")


def place(core, x, y, first, second, side):
    ahead = lax.bitwise_xor(y, jnp.where(core == 0, second, first))
    across = lax.bitwise_xor(x, jnp.where(core == 0, first, second))
    return ahead * side + across


def product_kernel(side, depth, other, groups, part, from_inputs, added, *refs):
    refs = list(refs)
    tokens = refs.pop(0)
    if from_inputs:
        grad, gate = refs.pop(0), refs.pop(0)
    else:
        left_ref = refs.pop(0)
    addend = refs.pop(0) if added else None
    outs = [refs.pop(0) for _ in groups]
    if from_inputs:
        left_ref = refs.pop(0)
    held, sems = refs[:2]
    core, x, y, z = position(side)
    half = 1 - core if other else core
    chips = side * side
    block = tokens.shape[1] // (2 * chips * depth)
    order = [(g, j, at) for g, group in enumerate(groups) for j, at in enumerate(group)]

    copies = []
    for i, (_, _, (f, s, q)) in enumerate(order):
        row = (lax.bitwise_xor(z, q) * 2 + half) * chips + place(half, x, y, f, s, side)
        start = pl.multiple_of(row * block, block)
        copies.append(
            pltpu.make_async_copy(tokens.at[:, pl.ds(start, block)], held.at[:, pl.ds(i * block, block)], sems.at[i])
        )
    if from_inputs:
        small = [pltpu.make_async_copy(a, refs[2].at[i], refs[3].at[i]) for i, a in enumerate((grad, gate))]
        for copy in small:
            copy.start()
    for copy in copies:
        copy.start()
    if from_inputs:
        for copy in small:
            copy.wait()
        v = refs[2][1].astype(jnp.float32)
        up = refs[2][0].astype(jnp.float32) * (v / (1.0 + jnp.exp(-v)))
        left_ref[...] = up.astype(jnp.bfloat16).T
    left = left_ref[part[0] : part[1], :]
    for copy in copies:
        copy.wait()
    for i, (g, j, _) in enumerate(order):
        value = jnp.dot(left, held[:, pl.ds(i * block, block)], preferred_element_type=jnp.float32)
        if added:
            value = value + addend[i].astype(jnp.float32)
        outs[g][j] = value.astype(jnp.bfloat16)


def products(tokens, ups, addend, other, groups, part, side, depth, block):
    from_inputs = len(ups) == 2
    token_rows, columns = ups[0].shape if from_inputs else ups[0].shape[::-1]
    count = sum(len(group) for group in groups)
    outs = [pltpu.VMEM((len(group), part[1] - part[0], block), jnp.bfloat16) for group in groups]
    if from_inputs:
        outs.append(pltpu.VMEM((columns, token_rows), jnp.bfloat16))
        tokens, ups = far_off(tokens), [far_off(u) for u in ups]
        extra = [pltpu.VMEM((2, *ups[0].shape), ups[0].dtype), pltpu.SemaphoreType.DMA((2,))]
    else:
        tokens, ups = near(tokens), [near(u) for u in ups]
        extra = []
    addends = [] if addend is None else [near(addend)]
    return pl.pallas_call(
        functools.partial(product_kernel, side, depth, other, groups, part, from_inputs, bool(addends)),
        out_shape=outs,
        in_specs=[HBM if from_inputs else VMEM] * (1 + len(ups)) + [VMEM] * len(addends),
        out_specs=[VMEM] * len(outs),
        scratch_shapes=[
            pltpu.VMEM((token_rows, count * block), jnp.bfloat16),
            pltpu.SemaphoreType.DMA((count,)),
            *extra,
        ],
        compiler_params=PARAMS,
        name="products",
    )(tokens, *ups, *addends)


def update_kernel(side, swapped, *refs):
    chips = side * side
    momentum, *pieces = refs[: 1 + chips]
    out, held, sems = refs[-3:]
    core, x, y, _ = position(side)
    block = momentum.shape[0] // (2 * chips)
    c = 1 - core if swapped else core
    copies = []
    for i in range(chips):
        start = (c * chips + place(c, x, y, i // side, i % side, side)) * block
        rows = pl.ds(pl.multiple_of(start, block), block)
        held[i] = 0.9 * momentum[rows, :] + pieces[i][...].astype(jnp.float32)
        copies.append(pltpu.make_async_copy(held.at[i], out.at[rows, :], sems.at[i]))
        copies[-1].start()
    for copy in copies:
        copy.wait()


def update(out, momentum, pieces, swapped, side):
    again = [] if out is None else [out]
    rows, columns = momentum.shape
    chips = len(pieces)
    return pl.pallas_call(
        functools.partial(update_kernel, side, swapped),
        out_shape=jax.ShapeDtypeStruct(momentum.shape, momentum.dtype),
        in_specs=[VMEM] * (1 + chips) + [HBM] * len(again),
        out_specs=HBM,
        input_output_aliases={1 + chips: 0} if again else {},
        scratch_shapes=[
            pltpu.VMEM((chips, rows // (2 * chips), columns), jnp.float32),
            pltpu.SemaphoreType.DMA((chips,)),
        ],
        compiler_params=PARAMS,
        name="update",
    )(near(momentum), *[near(p) for p in pieces], *again)


def turned_kernel(wide_parts, *refs):
    *parts, out = refs
    sums = []
    for group in (parts[:wide_parts], parts[wide_parts:]):
        value = group[0][0].astype(jnp.float32)
        for part in group[1:]:
            value += part[0].astype(jnp.float32)
        sums.append(value.astype(out.dtype))
    out[...] = jnp.concatenate(sums, axis=0).T


def turned(wide_parts, parts):
    columns = wide_parts[0].shape[1] + parts[0].shape[1]
    return pl.pallas_call(
        functools.partial(turned_kernel, len(wide_parts)),
        out_shape=pltpu.VMEM((parts[0].shape[2], columns), parts[0].dtype),
        in_specs=[VMEM] * (len(wide_parts) + len(parts)),
        out_specs=VMEM,
        compiler_params=PARAMS,
        name="turned",
    )(*[near(p) for p in (*wide_parts, *parts)])


def total(parts):
    out = parts[0].astype(jnp.float32)
    for part in parts[1:]:
        out = out + part.astype(jnp.float32)
    return out.astype(jnp.bfloat16)


def fast(side, depth, wide_columns, tokens, grad_hidden, gate_pre, momentum):
    nodes = 2 * side * side
    block = momentum.shape[0] // nodes
    columns = grad_hidden.shape[1]
    sides, depths = range(side), range(depth)
    wide_part, part = (0, wide_columns), (wide_columns, columns)

    def chip_pairs(first, second):
        pairs = []
        for n in range(nodes):
            core, x, y = n % 2, n // 2 % side, n // 2 // side
            dx, dy = (first, second) if core == 0 else (second, first)
            pairs.append((n, ((y ^ dy) * side + (x ^ dx)) * 2 + core))
        return pairs

    def swap(a):
        return lax.ppermute(a, "node", [(n, n ^ 1) for n in range(nodes)])

    def plane(a, first, second):
        return lax.ppermute(a, "node", chip_pairs(first, second))

    def along(a, q):
        return lax.ppermute(a, "local", [(i, i ^ q) for i in depths])

    def flat(groups):
        return [[at for group in groups for at in group]]

    def multiply(tokens, ups, addend, other, groups, of):
        return products(tokens, ups, addend, other, groups, of, side, depth, block)

    halving = [0]
    while len(halving) < depth:
        halving = [2 * q for q in halving] + [2 * q + 1 for q in halving]
    far = [[(f, s, q) for s in sides for q in halving] for f in range(1, side)]
    close = [[(0, s, q) for s in sides for q in halving]]
    wide = [[(f, s, q) for f in sides for s in sides] for q in depths]

    far_other, up_t = multiply(tokens, (grad_hidden, gate_pre), None, True, flat(far), part)
    far_got = swap(far_other)
    wide_other = multiply(tokens, (up_t,), None, True, flat(wide), wide_part)[0]
    wide_got = swap(wide_other)
    far_sum = multiply(tokens, (up_t,), far_got, False, far, part)
    held = [plane(a, f, 0) for f, a in enumerate(far_sum, 1)]
    wide_sum = multiply(tokens, (up_t,), wide_got, False, wide, wide_part)
    wide_held = [wide_sum[0]] + [along(wide_sum[q], q) for q in range(1, depth)]
    close_up = after(up_t, wide_other, *far_sum)
    close_other = multiply(tokens, (close_up,), None, True, close, part)[0]
    close_got = swap(close_other)
    held = [*multiply(tokens, (close_up,), close_got, False, close, part), *held]

    sent = [plane(total([a[s * depth : (s + 1) * depth] for a in held]), 0, s) for s in range(1, side)]
    held = held + sent
    step, left = 1, depth
    while left > 1:
        left //= 2
        sending = total([a[left : 2 * left] for a in held])
        if left == 1:
            wide_held = after(wide_held, sending)
        held = held + [along(sending, step)]
        step *= 2
    places = [(f, s) for f in sides for s in sides]
    blocks = [total([a[i : i + 1] for a in wide_held]) for i in range(len(places))]
    blocks = blocks[:1] + [plane(a, *at) for a, at in zip(blocks[1:], places[1:])]
    shard = turned(blocks, held)
    own = [shard if at == (0, 0) else plane(shard, *at) for at in places]
    out = update(None, momentum, own, False, side)
    return update(out, momentum, [swap(a) for a in own], True, side)


def plain(tokens, grad_hidden, gate_pre, momentum):
    up_grad = (grad_hidden.astype(jnp.float32) * jax.nn.silu(gate_pre.astype(jnp.float32))).astype(
        jnp.bfloat16
    )
    owned_rows = momentum.shape[0]
    columns = up_grad.shape[1]
    node_total = lax.psum_scatter(
        lax.dot_general(
            tokens, up_grad, (((0,), (0,)), ((), ())), preferred_element_type=jnp.float32
        ).astype(jnp.bfloat16),
        "local",
        scatter_dimension=0,
        tiled=True,
    )
    nodes = lax.axis_size("node")
    span = owned_rows // nodes
    reduced = jnp.sum(
        lax.all_to_all(
            node_total.reshape(nodes, span, columns),
            "node",
            split_axis=0,
            concat_axis=0,
            tiled=True,
        ).astype(jnp.float32),
        axis=0,
    )
    shard = reduced.astype(jnp.bfloat16)
    gathered = lax.all_gather(shard, "node", axis=0, tiled=True)
    return 0.9 * momentum + gathered.astype(jnp.float32)


def solution(mesh):
    nodes, depth = mesh.shape["node"], mesh.shape["local"]
    side = math.isqrt(nodes // 2)
    square = nodes == 2 * side * side and side & (side - 1) == 0 and depth & (depth - 1) == 0

    def per_device(tokens, grad_hidden, gate_pre, momentum):
        lanes = 128
        aligned = momentum.shape[0] % (nodes * lanes) == 0 and grad_hidden.shape[1] % lanes == 0
        if square and aligned:
            wide = grad_hidden.shape[1] * 7 // 16 // 16 * 16
            return fast(side, depth, wide, tokens, grad_hidden, gate_pre, momentum)
        return plain(tokens, grad_hidden, gate_pre, momentum)

    in_specs = (
        P(("node", "local"), None),
        P(("node", "local"), None),
        P(("node", "local"), None),
        P("local", None),
    )
    return jax.shard_map(
        per_device, mesh=mesh, in_specs=in_specs, out_specs=P("local", None), check_vma=False
    )
```
